32 devices in a mesh: space: 8 (over z, y), rep: 4 (over x, core).
Axes of the slice: x: 2, y: 2, z: 4, core: 2. Of those that a mesh axis runs over, the one named last changes fastest.
Arguments:
- features: bfloat16 [128, 64, 512], P(('space', 'rep')), may hold values from -6 to 6
- neighbours: int32 [128, 27], P(('space', 'rep')), may hold values from -1 to 7, as said below
- counts: int32 [32], P(('space', 'rep')), may hold values from 1 to 4, as said below
- cotangent: bfloat16 [128, 64, 128], P(('space', 'rep')), may hold values from -0.06591797 to 0.06591797
- conv_weight: bfloat16 [27, 64, 64], replicated, may hold values from -0.15625 to 0.15625
- down_weight: bfloat16 [8, 128, 64], replicated, may hold values from -0.25 to 0.25
Outputs:
- hidden: bfloat16 [128, 64, 512], P(('space', 'rep'))
- conv_grad: float32 [27, 64, 64], replicated
- down_grad: float32 [8, 128, 64], replicated
The draws below stay inside these ranges and needn't reach their ends.
Inputs may be any that keep to these rules, and one draw needn't show every extreme that they name: `counts`: in every tile, of the two strips s and s + 4 at most one has more than 2 occupied blocks; some strip has exactly 4 and some exactly 2. Only live slots name neighbours, and they name only live slots; strip 0 names nothing below and the last strip nothing above.
All inputs are finite; a program needn't handle non-finite values.
Results may differ from the reference program's by a relative error of at most 0.0029.
Values may be sent and summed in bfloat16 or wider, within the bound.
No kernel may reach another device: no remote copies, remote signals or barrier semaphores. Data moves between devices by JAX's collectives and lax.ppermute only.
A program may use at most 64 MiB of HBM per device.

```python
import jax
import jax.numpy as jnp
from jax import lax

C = 64
C2 = 128
SLOTS = 4
BLOCKS = 128
N_SPACE = 8
N_REP = 4


def pair_counts(key):
    half_space = N_SPACE // 2
    key_side, key_heavy, key_light = jax.random.split(jax.random.fold_in(key, 7), 3)
    heavy_side = jax.random.randint(key_side, (half_space, N_REP), 0, 2)
    heavy_count = jax.random.randint(key_heavy, (half_space, N_REP), SLOTS // 2 + 1, SLOTS + 1)
    light_count = jax.random.randint(key_light, (half_space, N_REP), 1, SLOTS // 2 + 1)
    heavy_count = heavy_count.at[0, 0].set(SLOTS)
    light_count = light_count.at[0, 0].set(SLOTS // 2)
    first_half = jnp.where(heavy_side == 1, heavy_count, light_count)
    second_half = jnp.where(heavy_side == 1, light_count, heavy_count)
    return jnp.concatenate([first_half, second_half], 0).astype(jnp.int32)


def draw_counts(key, part):
    return pair_counts(key).reshape(N_SPACE * N_REP)


def draw_neighbours(key, part):
    strip_counts = pair_counts(key)
    key_bits, key_present, key_side = jax.random.split(jax.random.fold_in(key, 13), 3)
    shape = (N_SPACE, N_REP, SLOTS, 27)
    random_bits = jax.random.randint(key_bits, shape, 0, 1 << 20)
    present = jax.random.randint(key_present, shape, 0, 5) < 3
    side_pick = jax.random.randint(key_side, shape, 0, 2)
    zero_row = jnp.zeros((1, N_REP), jnp.int32)
    own_count = strip_counts[:, :, None, None]
    prev_count = jnp.concatenate([zero_row, strip_counts[:-1]], 0)[:, :, None, None]
    next_count = jnp.concatenate([strip_counts[1:], zero_row], 0)[:, :, None, None]
    column = jnp.arange(27, dtype=jnp.int32)
    use_prev = (column < 9) & (side_pick == 1) & (prev_count > 0)
    use_next = (column >= 18) & (side_pick == 1) & (next_count > 0)
    own_index = random_bits % own_count
    prev_index = SLOTS + random_bits % jnp.maximum(prev_count, 1)
    next_index = SLOTS + random_bits % jnp.maximum(next_count, 1)
    chosen = jnp.where(use_prev, prev_index, jnp.where(use_next, next_index, own_index))
    slot_index = jnp.arange(SLOTS, dtype=jnp.int32)[None, None, :, None]
    live_mask = slot_index < own_count
    chosen = jnp.where(present & live_mask, chosen, -1)
    chosen = jnp.where((column == 13) & live_mask, slot_index, chosen)
    return chosen.reshape(N_SPACE * N_REP * SLOTS, 27).astype(jnp.int32)


def level_of(stream_key, shape, shards, least, top_value):
    def one(dim, shards_of):
        draws = jax.random.uniform(jax.random.fold_in(jax.random.fold_in(stream_key, 6), dim), (shards_of,), jnp.float32, least / len(shards), top_value / len(shards))
        return jnp.repeat(jnp.exp(draws), shape[dim] // shards_of).reshape((-1,) + (1,) * (len(shape) - dim - 1))

    level = one(*shards[0])
    for cut in shards[1:]:
        level = level * one(*cut)
    return level


def noise(key, shape, width, bound, cuts=(), kind=jnp.bfloat16):
    result = width * jax.random.normal(key, shape, jnp.float32)
    if cuts:
        result = result * level_of(key, shape, cuts, -0.22, 0.18)
    return jnp.clip(result, -bound, bound).astype(kind)


def setup_inputs(seed: int = 0) -> dict:
    key_of = jax.random.split(jax.random.key(seed), 7)
    features = noise(key_of[0], (BLOCKS, C, 512), 1.0, 6.0, ((0, 32),))
    neighbours = draw_neighbours(jax.random.fold_in(key_of[6], 71), 0)
    counts = draw_counts(jax.random.fold_in(key_of[6], 71), 0)
    cotangent = noise(key_of[3], (BLOCKS, 64, C2), (0.125 / (N_SPACE * N_REP * SLOTS) ** 0.5), 0.06591797, ((0, 32),))
    conv_weight = noise(key_of[4], (27, C, C), (27 * C) ** -0.5, 0.15625)
    down_weight = noise(key_of[5], (8, C2, C), (8 * C) ** -0.5, 0.25)
    return {"features": features, "neighbours": neighbours, "counts": counts, "cotangent": cotangent, "conv_weight": conv_weight, "down_weight": down_weight}


def plane_slice(offset):
    if offset < 0:
        return slice(7, 8)
    if offset > 0:
        return slice(0, 1)
    return slice(0, 8)


def take_rows(source_table, index_rows):
    padding = jnp.zeros((1,) + source_table.shape[1:], source_table.dtype)
    extended = jnp.concatenate([source_table, padding], 0)
    safe_index = jnp.where(index_rows < 0, source_table.shape[0], index_rows).astype(jnp.int32)
    return jnp.take(extended, safe_index, axis=0)


def build_padded(features_live, prev_upper, next_lower, neighbours):
    count_rows, channels = features_live.shape[0], features_live.shape[1]
    blocks = features_live.reshape(count_rows, channels, 8, 8, 8)
    low_table = jnp.concatenate([blocks[:, :, 7:8], prev_upper.reshape(-1, channels, 1, 8, 8)], 0)
    high_table = jnp.concatenate([blocks[:, :, 0:1], next_lower.reshape(-1, channels, 1, 8, 8)], 0)
    layers = []
    for step_x, source_table in ((-1, low_table), (0, blocks), (1, high_table)):
        row_list = []
        for step_y in (-1, 0, 1):
            tile_list = []
            for step_z in (-1, 0, 1):
                column = (step_x + 1) * 9 + (step_y + 1) * 3 + step_z + 1
                if column == 13:
                    tile_list.append(blocks)
                else:
                    piece = source_table[:, :, :, plane_slice(step_y), plane_slice(step_z)]
                    tile_list.append(take_rows(piece, neighbours[:, column]))
            row_list.append(jnp.concatenate(tile_list, 4))
        layers.append(jnp.concatenate(row_list, 3))
    return jnp.concatenate(layers, 2)


def block_section(padded, grads_in, conv_weight, down_weight):
    count_rows, channels = padded.shape[0], padded.shape[1]
    out_channels = down_weight.shape[1]

    def shifted_at(column):
        step_x, step_y, step_z = column // 9 - 1, (column // 3) % 3 - 1, column % 3 - 1
        window = padded[:, :, 1 + step_x:9 + step_x, 1 + step_y:9 + step_y, 1 + step_z:9 + step_z]
        return window.reshape(count_rows, channels, 512).astype(jnp.float32)

    weights = conv_weight.astype(jnp.float32)
    pre_act = jnp.zeros((count_rows, channels, 512), jnp.float32)
    for column in range(27):
        pre_act = pre_act + jnp.einsum("oc,bcv->bov", weights[column], shifted_at(column))
    hidden = jnp.maximum(pre_act, 0.0).astype(jnp.bfloat16)
    hidden_cells = hidden.reshape(count_rows, channels, 4, 2, 4, 2, 4, 2).astype(jnp.float32)
    grid_grads = grads_in.reshape(count_rows, 4, 4, 4, out_channels).astype(jnp.float32)
    down_grad = jnp.einsum("bcxiyjzk,bxyzo->ijkoc", hidden_cells, grid_grads).reshape(8, out_channels, channels)
    kernel = down_weight.reshape(2, 2, 2, out_channels, channels).astype(jnp.float32)
    hidden_grad = jnp.einsum("ijkoc,bxyzo->bcxiyjzk", kernel, grid_grads).reshape(count_rows, channels, 512)
    act_grad = jnp.where(pre_act > 0, hidden_grad, 0.0).astype(jnp.bfloat16).astype(jnp.float32)
    conv_grad = jnp.stack([jnp.einsum("bov,bcv->oc", act_grad, shifted_at(column)) for column in range(27)])
    return hidden, conv_grad, down_grad


def reference(features, neighbours, counts, cotangent, conv_weight, down_weight):
    feats_all = features.reshape(N_SPACE, N_REP, SLOTS, C, 512)
    slot_index = jnp.arange(SLOTS, dtype=jnp.int32)
    live_mask = slot_index[None, None, :] < counts.reshape(N_SPACE, N_REP)[:, :, None]
    features_live = jnp.where(live_mask[..., None, None], feats_all, jnp.zeros_like(feats_all))
    grads_all = cotangent.reshape(N_SPACE, N_REP, SLOTS, 64, C2)
    grads_live = jnp.where(live_mask[..., None, None], grads_all, jnp.zeros_like(grads_all))
    links = neighbours.reshape(N_SPACE, N_REP, SLOTS, 27)
    upper = features_live[..., 448:]
    lower = features_live[..., :64]
    zero_plane = jnp.zeros_like(upper[:1])
    prev_upper = jnp.concatenate([zero_plane, upper[:-1]], 0)
    next_lower = jnp.concatenate([lower[1:], zero_plane], 0)

    def one_tile(feats_one, prev_one, next_one, links_one, grads_one):
        padded = build_padded(feats_one, prev_one, next_one, links_one)
        return block_section(padded, grads_one, conv_weight, down_weight)

    def one_strip(items):
        hidden, conv_part, down_part = jax.vmap(one_tile)(*items)
        return hidden, jnp.sum(conv_part, 0), jnp.sum(down_part, 0)

    hidden, conv_part, down_part = lax.map(one_strip, (features_live, prev_upper, next_lower, links, grads_live))
    return hidden.reshape(BLOCKS, C, 512), jnp.sum(conv_part, 0), jnp.sum(down_part, 0)
```

```python
import functools

import jax
import jax.numpy as jnp
from jax import lax
from jax.experimental import pallas as pl
from jax.experimental.pallas import tpu as pltpu
from jax.sharding import PartitionSpec as P


F32 = jnp.float32
BF16 = jnp.bfloat16
LANES = 128


def dot(a, b, dims):
    return lax.dot_general(a, b, (dims, ((), ())), preferred_element_type=F32)


def lane_iota(shape):
    return lax.broadcasted_iota(jnp.int32, shape, len(shape) - 1)


def doubled(rows):
    return jnp.concatenate([rows, rows], 0).astype(F32).T


def section_kernel(
    nb_ref, cnt_ref, feat_ref, prev_ref, next_ref, cot_ref, cw_ref, dw_ref,
    hid_ref, grad_ref,
    t0_ref, tl_ref, th_ref, sa_ref, sb_ref, wn_ref, hp_ref, as_ref,
):
    slots, ch, vox = feat_ref.shape
    half = ch

    t0_ref[slots] = jnp.zeros(t0_ref.shape[1:], F32)
    tl_ref[2 * slots] = jnp.zeros(tl_ref.shape[1:], F32)
    th_ref[2 * slots] = jnp.zeros(th_ref.shape[1:], F32)
    for j in range(slots):
        block = doubled(feat_ref[j]).reshape(8, 8, 8, LANES)
        t0_ref[j] = block
        tl_ref[j] = block[7]
        th_ref[j] = block[0]
        tl_ref[slots + j] = doubled(prev_ref[j])[64:].reshape(8, 8, LANES)
        th_ref[slots + j] = doubled(next_ref[j])[:64].reshape(8, 8, LANES)

    low_lanes = lane_iota((ch, LANES)) < half
    for iy in range(3):
        for ix in range(3):
            parts = []
            for iz in range(3):
                w = cw_ref[ix * 9 + iy * 3 + iz].astype(F32)
                parts.append(jnp.concatenate([w, jnp.zeros_like(w)], 1))
            both = jnp.where(low_lanes, parts[0], pltpu.roll(parts[1], half, 1))
            wn_ref[iy, pl.ds(ix * ch, ch), pl.ds(0, LANES)] = both.astype(BF16)
            wn_ref[iy, pl.ds(ix * ch, ch), pl.ds(LANES, LANES)] = parts[2].astype(BF16)

    row = lax.broadcasted_iota(jnp.int32, (vox, LANES), 0)
    t, u = row // 64, row % 64
    voxel = (
        64 * (2 * (u // 16) + t // 4)
        + 8 * (2 * (u // 4 % 4) + t // 2 % 2)
        + 2 * (u % 4) + t % 2
    )
    lane = lane_iota((vox, LANES))
    onehot = jnp.concatenate(
        [
            jnp.where(voxel == lane + q * LANES, 1.0, 0.0).astype(BF16)
            for q in range(vox // LANES)
        ],
        1,
    )

    cot = cot_ref[...].reshape(slots * 64, LANES)
    taps = dw_ref.shape[0]
    dwt = jnp.concatenate([dw_ref[t].astype(F32).T.astype(BF16) for t in range(taps)], 0)
    hg = dot(dwt, cot, ((1,), (1,)))
    low = lane_iota((ch, LANES)) < half

    def regroup(blocks, outer, inner):
        rows = []
        for j in range(inner):
            tiles = []
            for m in range(outer // 2):
                a = blocks[2 * m * ch : (2 * m + 1) * ch, j // 2 * LANES : (j // 2 + 1) * LANES]
                b = blocks[(2 * m + 1) * ch : (2 * m + 2) * ch, j // 2 * LANES : (j // 2 + 1) * LANES]
                if j % 2 == 0:
                    tiles.append(jnp.where(low, a, pltpu.roll(b, half, 1)))
                else:
                    tiles.append(jnp.where(low, pltpu.roll(a, half, 1), b))
            rows.append(jnp.concatenate(tiles, 1))
        return jnp.concatenate(rows, 0)

    hg = regroup(hg, taps, slots).astype(BF16)
    hp_ref[...] = dot(hg, onehot, ((1,), (0,)))

    zi = lax.broadcasted_iota(jnp.int32, (10, 8, LANES), 1)
    li = lane_iota((10, 8, LANES))
    for j in range(slots):
        def source(col):
            n = nb_ref[j, col]
            return jnp.where(n < 0, slots if 9 <= col < 18 else 2 * slots, n)

        centre = jnp.where(j < cnt_ref[0], j, slots)
        for xp in range(10):
            ox = -1 if xp == 0 else (1 if xp == 9 else 0)
            shifted = []
            for oz in (-1, 0, 1):
                pieces = []
                for oy in (-1, 0, 1):
                    col = (ox + 1) * 9 + (oy + 1) * 3 + oz + 1
                    n = centre if col == 13 else source(col)
                    ys = slice(7, 8) if oy < 0 else (slice(0, 1) if oy > 0 else slice(0, 8))
                    if ox == 0:
                        pieces.append(t0_ref[n, xp - 1, ys])
                    elif ox < 0:
                        pieces.append(tl_ref[n, ys])
                    else:
                        pieces.append(th_ref[n, ys])
                shifted.append(jnp.concatenate(pieces, 0))
            below, here, above = shifted
            zm = pltpu.roll(jnp.where(zi == 7, below, here), 1, 1)
            zp = pltpu.roll(jnp.where(zi == 0, above, here), 7, 1)
            s01 = jnp.where(li < half, zm, here)
            sa_ref[j, xp, :, pl.ds(0, LANES)] = s01.reshape(80, LANES).astype(BF16)
            sa_ref[j, xp, :, pl.ds(LANES, LANES)] = zp.reshape(80, LANES).astype(BF16)
            sb_ref[j, xp, :, pl.ds(0, LANES)] = s01[1:9].reshape(64, LANES).astype(BF16)
            sb_ref[j, xp, :, pl.ds(LANES, LANES)] = zp[1:9].reshape(64, LANES).astype(BF16)

    def window(iy, first, count):
        if iy == 1:
            s = sb_ref[pl.ds(first, count)]
        else:
            s = sa_ref[pl.ds(first, count), :, pl.ds(8 * iy, 64)]
        return s.reshape(count * 640, 2 * LANES)

    zero = jnp.zeros((ch, LANES), F32)
    for j in range(slots):
        out = dot(window(0, j, 1), wn_ref[0], ((1,), (1,)))
        out = out + dot(window(1, j, 1), wn_ref[1], ((1,), (1,)))
        out = out + dot(window(2, j, 1), wn_ref[2], ((1,), (1,)))
        first = out[:, :LANES]
        second = out[:, LANES:]
        pre = (
            first[:vox]
            + pltpu.roll(first[64 : 64 + vox], half, 1)
            + jnp.concatenate([second[128 : 128 + vox], jnp.zeros((vox, LANES - ch), F32)], 1)
        )
        pre = pre.T[:ch]
        hid_ref[j] = jnp.maximum(pre, 0.0).astype(BF16)
        act = jnp.where(pre > 0, hp_ref[pl.ds(j * ch, ch), :], 0.0)
        lead = jnp.concatenate([act, zero], 1)
        as_ref[pl.ds(0, ch), pl.ds(j * 640, 640)] = lead.astype(BF16)
        as_ref[pl.ds(ch, ch), pl.ds(j * 640, 640)] = pltpu.roll(lead, half, 1).astype(BF16)
        as_ref[pl.ds(2 * ch, ch), pl.ds(j * 640, 640)] = jnp.concatenate([zero, act], 1).astype(BF16)

    hidden = hid_ref[...].reshape(slots * ch, vox)
    hperm = dot(hidden, onehot, ((1,), (1,)))
    hperm = regroup(hperm, slots, taps).astype(BF16)
    cott = cot.astype(F32).T.astype(BF16)
    down = dot(cott, hperm, ((1,), (1,)))
    base = 3 * 3 * ch + 3 * ch + 3 * ch // 2
    for q in range(taps // 2):
        grad_ref[pl.ds(base + q * 128, 128), :] = down[:, q * LANES : (q + 1) * LANES]

    tails = []
    for iy in range(3):
        g = dot(as_ref[...], window(iy, 0, slots), ((1,), (0,)))
        grad_ref[pl.ds(iy * 3 * ch, 3 * ch), :] = g[:, :LANES]
        tails.append(g[:, LANES:])
    wide = lane_iota((3 * ch, LANES)) < half
    grad_ref[pl.ds(9 * ch, 3 * ch), :] = jnp.where(wide, tails[0], tails[1])
    hrows = 3 * ch // 2
    grad_ref[pl.ds(12 * ch, hrows), :] = jnp.where(wide[:hrows], tails[2][:hrows], tails[2][hrows:])
    used = base + taps * ch
    grad_ref[pl.ds(used, grad_ref.shape[0] - used), :] = jnp.zeros((grad_ref.shape[0] - used, LANES), F32)


def unpack_kernel(x_ref, conv_ref, down_ref):
    taps, outs, ch = down_ref.shape
    half = ch
    base = 9 * ch + 3 * ch + 3 * ch // 2

    def put(ref, k, tile, upper):
        if upper:
            tile = pltpu.roll(tile, half, 1)
        ref[k] = tile[:, :ch]

    for iy in range(3):
        for ix in range(3):
            tile = x_ref[pl.ds(iy * 3 * ch + ix * ch, ch), :]
            put(conv_ref, ix * 9 + iy * 3, tile, False)
            put(conv_ref, ix * 9 + iy * 3 + 1, tile, True)
    for ix in range(3):
        tile = x_ref[pl.ds(9 * ch + ix * ch, ch), :]
        put(conv_ref, ix * 9 + 2, tile, False)
        put(conv_ref, ix * 9 + 5, tile, True)
    tail = x_ref[pl.ds(12 * ch, 3 * ch // 2), :]
    tail = jnp.concatenate([tail, pltpu.roll(tail, half, 1)], 0)
    for ix in range(3):
        conv_ref[ix * 9 + 8] = tail[ix * ch : (ix + 1) * ch, :ch]
    for q in range(taps // 2):
        tile = x_ref[pl.ds(base + q * outs, outs), :]
        put(down_ref, 2 * q, tile, False)
        put(down_ref, 2 * q + 1, tile, True)


def from_behind(block, axis, distance):
    devices = range(lax.axis_size(axis))
    route = [(i - distance, i) for i in devices if i - distance in devices]
    return lax.ppermute(block, axis, route)


def partner(block, axis, bit):
    route = [(i, i ^ (1 << bit)) for i in range(lax.axis_size(axis))]
    return lax.ppermute(block, axis, route)


def halves(block, axis, bit):
    side = lax.axis_index(axis) >> bit & 1
    rows = block.shape[0] // 2
    low, high = block[:rows], block[rows:]
    keep = jnp.where(side == 1, high, low)
    give = jnp.where(side == 1, low, high)
    return keep, give, side


def reduce_all(block):
    scatter = [("rep", 0), ("rep", 1), ("space", 0)]
    whole = [("space", b) for b in range(1, lax.axis_size("space").bit_length() - 1)]
    whole += [("rep", b) for b in range(2, lax.axis_size("rep").bit_length() - 1)]
    for axis, bit in scatter:
        keep, give, _ = halves(block, axis, bit)
        block = keep + partner(give, axis, bit)
    for axis, bit in whole:
        block = block + partner(block, axis, bit)
    for axis, bit in reversed(scatter):
        other = partner(block, axis, bit)
        side = lax.axis_index(axis) >> bit & 1
        block = jnp.where(
            side == 1, jnp.concatenate([other, block], 0), jnp.concatenate([block, other], 0)
        )
    return block


def body(features, neighbours, counts, cotangent, conv_weight, down_weight):
    slots, ch, vox = features.shape
    prev_upper = from_behind(features[:, :, vox - LANES :], "space", 1)
    next_lower = from_behind(features[:, :, :LANES], "space", -1)
    vmem = pl.BlockSpec(memory_space=pltpu.VMEM)
    smem = pl.BlockSpec(memory_space=pltpu.SMEM)
    taps, outs, _ = down_weight.shape
    total = conv_weight.size + down_weight.size
    rows = -(-total // (LANES * 128)) * 128
    hidden, grads = pl.pallas_call(
        section_kernel,
        out_shape=(
            jax.ShapeDtypeStruct((slots, ch, vox), BF16),
            jax.ShapeDtypeStruct((rows, LANES), F32),
        ),
        in_specs=[smem, smem] + [vmem] * 6,
        out_specs=(vmem, vmem),
        scratch_shapes=[
            pltpu.VMEM((slots + 1, 8, 8, 8, LANES), F32),
            pltpu.VMEM((2 * slots + 1, 8, 8, LANES), F32),
            pltpu.VMEM((2 * slots + 1, 8, 8, LANES), F32),
            pltpu.VMEM((slots, 10, 80, 2 * LANES), BF16),
            pltpu.VMEM((slots, 10, 64, 2 * LANES), BF16),
            pltpu.VMEM((3, 3 * ch, 2 * LANES), BF16),
            pltpu.VMEM((slots * ch, vox), F32),
            pltpu.VMEM((3 * ch, slots * 640), BF16),
        ],
        name="section",
    )(neighbours, counts, features, prev_upper, next_lower, cotangent, conv_weight, down_weight)
    grads = reduce_all(grads)
    conv_grad, down_grad = pl.pallas_call(
        unpack_kernel,
        out_shape=(
            jax.ShapeDtypeStruct(conv_weight.shape, F32),
            jax.ShapeDtypeStruct(down_weight.shape, F32),
        ),
        in_specs=[vmem],
        out_specs=(vmem, vmem),
        name="unpack",
    )(grads)
    return hidden, conv_grad, down_grad


def solution(mesh):
    return jax.shard_map(
        body,
        mesh=mesh,
        in_specs=(
            P(("space", "rep"), None, None),
            P(("space", "rep"), None),
            P(("space", "rep")),
            P(("space", "rep"), None, None),
            P(),
            P(),
        ),
        out_specs=(P(("space", "rep"), None, None), P(), P()),
        check_vma=False,
    )
```

```python
import functools

import jax
import jax.numpy as jnp
from jax import lax
from jax.experimental import pallas as pl
from jax.experimental.pallas import tpu as pltpu
from jax.sharding import PartitionSpec as P


F32 = jnp.float32
BF16 = jnp.bfloat16
LANES = 128


def dot(a, b, dims):
    return lax.dot_general(a, b, (dims, ((), ())), preferred_element_type=F32)


def lane_iota(shape):
    return lax.broadcasted_iota(jnp.int32, shape, len(shape) - 1)


def doubled(rows):
    return jnp.concatenate([rows, rows], 0).astype(F32).T


def section_kernel(
    nb_ref, cnt_ref, place_ref, feat_ref, near_ref, far_ref, cot_ref, cw_ref, dw_ref,
    hid_ref, keep_a_ref, give_a_ref, keep_b_ref, give_b_ref,
    t0_ref, tl_ref, th_ref, sa_ref, sb_ref, wn_ref, hp_ref, as_ref, grad_ref,
):
    slots, ch, vox = feat_ref.shape
    half = ch
    odd = place_ref[0]
    core = place_ref[1]

    t0_ref[slots] = jnp.zeros(t0_ref.shape[1:], F32)
    tl_ref[2 * slots] = jnp.zeros(tl_ref.shape[1:], F32)
    th_ref[2 * slots] = jnp.zeros(th_ref.shape[1:], F32)
    for j in range(slots):
        block = doubled(feat_ref[j]).reshape(8, 8, 8, LANES)
        t0_ref[j] = block
        tl_ref[j] = block[7]
        th_ref[j] = block[0]
        near, far = doubled(near_ref[j]), doubled(far_ref[j])
        before = jnp.where(odd == 1, near, far)
        after = jnp.where(odd == 1, far, near)
        tl_ref[slots + j] = before[64:].reshape(8, 8, LANES)
        th_ref[slots + j] = after[:64].reshape(8, 8, LANES)

    low_lanes = lane_iota((ch, LANES)) < half
    for iy in range(3):
        for ix in range(3):
            parts = []
            for iz in range(3):
                w = cw_ref[ix * 9 + iy * 3 + iz].astype(F32)
                parts.append(jnp.concatenate([w, jnp.zeros_like(w)], 1))
            both = jnp.where(low_lanes, parts[0], pltpu.roll(parts[1], half, 1))
            wn_ref[iy, pl.ds(ix * ch, ch), pl.ds(0, LANES)] = both.astype(BF16)
            wn_ref[iy, pl.ds(ix * ch, ch), pl.ds(LANES, LANES)] = parts[2].astype(BF16)

    row = lax.broadcasted_iota(jnp.int32, (vox, LANES), 0)
    t, u = row // 64, row % 64
    voxel = (
        64 * (2 * (u // 16) + t // 4)
        + 8 * (2 * (u // 4 % 4) + t // 2 % 2)
        + 2 * (u % 4) + t % 2
    )
    lane = lane_iota((vox, LANES))
    onehot = jnp.concatenate(
        [
            jnp.where(voxel == lane + q * LANES, 1.0, 0.0).astype(BF16)
            for q in range(vox // LANES)
        ],
        1,
    )

    cot = cot_ref[...].reshape(slots * 64, LANES)
    taps = dw_ref.shape[0]
    hg = dot(dw_ref[...].reshape(taps * ch, LANES), cot, ((1,), (1,)))
    low = lane_iota((ch, LANES)) < half

    def regroup(blocks, outer, inner):
        rows = []
        for j in range(inner):
            tiles = []
            for m in range(outer // 2):
                a = blocks[2 * m * ch : (2 * m + 1) * ch, j // 2 * LANES : (j // 2 + 1) * LANES]
                b = blocks[(2 * m + 1) * ch : (2 * m + 2) * ch, j // 2 * LANES : (j // 2 + 1) * LANES]
                if j % 2 == 0:
                    tiles.append(jnp.where(low, a, pltpu.roll(b, half, 1)))
                else:
                    tiles.append(jnp.where(low, pltpu.roll(a, half, 1), b))
            rows.append(jnp.concatenate(tiles, 1))
        return jnp.concatenate(rows, 0)

    hg = regroup(hg, taps, slots).astype(BF16)
    hp_ref[...] = dot(hg, onehot, ((1,), (0,)))

    zi = lax.broadcasted_iota(jnp.int32, (10, 8, LANES), 1)
    li = lane_iota((10, 8, LANES))
    for j in range(slots):
        def source(col):
            n = nb_ref[j, col]
            return jnp.where(n < 0, slots if 9 <= col < 18 else 2 * slots, n)

        centre = jnp.where(j < cnt_ref[0], j, slots)
        for xp in range(10):
            ox = -1 if xp == 0 else (1 if xp == 9 else 0)
            shifted = []
            for oz in (-1, 0, 1):
                pieces = []
                for oy in (-1, 0, 1):
                    col = (ox + 1) * 9 + (oy + 1) * 3 + oz + 1
                    n = centre if col == 13 else source(col)
                    ys = slice(7, 8) if oy < 0 else (slice(0, 1) if oy > 0 else slice(0, 8))
                    if ox == 0:
                        pieces.append(t0_ref[n, xp - 1, ys])
                    elif ox < 0:
                        pieces.append(tl_ref[n, ys])
                    else:
                        pieces.append(th_ref[n, ys])
                shifted.append(jnp.concatenate(pieces, 0))
            below, here, above = shifted
            zm = pltpu.roll(jnp.where(zi == 7, below, here), 1, 1)
            zp = pltpu.roll(jnp.where(zi == 0, above, here), 7, 1)
            s01 = jnp.where(li < half, zm, here)
            sa_ref[j, xp, :, pl.ds(0, LANES)] = s01.reshape(80, LANES).astype(BF16)
            sa_ref[j, xp, :, pl.ds(LANES, LANES)] = zp.reshape(80, LANES).astype(BF16)
            sb_ref[j, xp, :, pl.ds(0, LANES)] = s01[1:9].reshape(64, LANES).astype(BF16)
            sb_ref[j, xp, :, pl.ds(LANES, LANES)] = zp[1:9].reshape(64, LANES).astype(BF16)

    def window(iy, first, count):
        if iy == 1:
            s = sb_ref[pl.ds(first, count)]
        else:
            s = sa_ref[pl.ds(first, count), :, pl.ds(8 * iy, 64)]
        return s.reshape(count * 640, 2 * LANES)

    zero = jnp.zeros((ch, LANES), F32)
    for j in range(slots):
        out = dot(window(0, j, 1), wn_ref[0], ((1,), (1,)))
        out = out + dot(window(1, j, 1), wn_ref[1], ((1,), (1,)))
        out = out + dot(window(2, j, 1), wn_ref[2], ((1,), (1,)))
        first = out[:, :LANES]
        second = out[:, LANES:]
        pre = (
            first[:vox]
            + pltpu.roll(first[64 : 64 + vox], half, 1)
            + jnp.concatenate([second[128 : 128 + vox], jnp.zeros((vox, LANES - ch), F32)], 1)
        )
        pre = pre.T[:ch]
        hid_ref[j] = jnp.maximum(pre, 0.0).astype(BF16)
        act = jnp.where(pre > 0, hp_ref[pl.ds(j * ch, ch), :], 0.0)
        lead = jnp.concatenate([act, zero], 1)
        as_ref[pl.ds(0, ch), pl.ds(j * 640, 640)] = lead.astype(BF16)
        as_ref[pl.ds(ch, ch), pl.ds(j * 640, 640)] = pltpu.roll(lead, half, 1).astype(BF16)
        as_ref[pl.ds(2 * ch, ch), pl.ds(j * 640, 640)] = jnp.concatenate([zero, act], 1).astype(BF16)

    hidden = hid_ref[...].reshape(slots * ch, vox)
    hperm = dot(hidden, onehot, ((1,), (1,)))
    hperm = regroup(hperm, slots, taps).astype(BF16)
    base = 3 * 3 * ch + 3 * ch + 3 * ch // 2
    grad_ref[pl.ds(base, taps * ch), :] = dot(hperm, cot, ((1,), (0,)))

    tails = []
    for iy in range(3):
        g = dot(as_ref[...], window(iy, 0, slots), ((1,), (0,)))
        grad_ref[pl.ds(iy * 3 * ch, 3 * ch), :] = g[:, :LANES]
        tails.append(g[:, LANES:])
    wide = lane_iota((3 * ch, LANES)) < half
    grad_ref[pl.ds(9 * ch, 3 * ch), :] = jnp.where(wide, tails[0], tails[1])
    hrows = 3 * ch // 2
    grad_ref[pl.ds(12 * ch, hrows), :] = jnp.where(wide[:hrows], tails[2][:hrows], tails[2][hrows:])
    used = base + taps * ch
    grad_ref[pl.ds(used, grad_ref.shape[0] - used), :] = jnp.zeros((grad_ref.shape[0] - used, LANES), F32)

    rows = keep_a_ref.shape[0]
    mine, theirs = pl.multiple_of(core * rows, 8), pl.multiple_of((1 - core) * rows, 8)
    keep_a_ref[...] = grad_ref[pl.ds(mine, rows), :]
    give_a_ref[...] = grad_ref[pl.ds(theirs, rows), :]
    keep_b_ref[...] = grad_ref[pl.ds(2 * rows + mine, rows), :]
    give_b_ref[...] = grad_ref[pl.ds(2 * rows + theirs, rows), :]


def unpack_kernel(place_ref, mine_a, other_a, mine_b, other_b, conv_ref, down_ref, x_ref):
    taps, ch, outs = down_ref.shape
    half = ch
    core = place_ref[1]
    rows = mine_a.shape[0]
    mine, theirs = pl.multiple_of(core * rows, 8), pl.multiple_of((1 - core) * rows, 8)
    x_ref[pl.ds(mine, rows), :] = mine_a[...]
    x_ref[pl.ds(theirs, rows), :] = other_a[...]
    x_ref[pl.ds(2 * rows + mine, rows), :] = mine_b[...]
    x_ref[pl.ds(2 * rows + theirs, rows), :] = other_b[...]
    base = 9 * ch + 3 * ch + 3 * ch // 2

    def put(ref, k, tile, upper):
        if upper:
            tile = pltpu.roll(tile, half, 1)
        ref[k] = tile[:, :ch]

    for iy in range(3):
        for ix in range(3):
            tile = x_ref[pl.ds(iy * 3 * ch + ix * ch, ch), :]
            put(conv_ref, ix * 9 + iy * 3, tile, False)
            put(conv_ref, ix * 9 + iy * 3 + 1, tile, True)
    for ix in range(3):
        tile = x_ref[pl.ds(9 * ch + ix * ch, ch), :]
        put(conv_ref, ix * 9 + 2, tile, False)
        put(conv_ref, ix * 9 + 5, tile, True)
    tail = x_ref[pl.ds(12 * ch, 3 * ch // 2), :]
    tail = jnp.concatenate([tail, pltpu.roll(tail, half, 1)], 0)
    for ix in range(3):
        conv_ref[ix * 9 + 8] = tail[ix * ch : (ix + 1) * ch, :ch]
    down_ref[...] = x_ref[pl.ds(base, taps * ch), :].reshape(taps, ch, outs)


def axis_bits(axis):
    return [(axis, b) for b in range(lax.axis_size(axis).bit_length() - 1)]


def routes():
    first = axis_bits("rep")[1:] + axis_bits("space")
    second = list(first)
    for i in range(0, len(second) - 1, 2):
        second[i], second[i + 1] = second[i + 1], second[i]
    return first, second


def other_core(block):
    return lax.ppermute(block, "rep", [(i, i ^ 1) for i in range(lax.axis_size("rep"))])


def swapped(block, stage):
    count = lax.axis_size("rep")
    route = []
    for s in range(lax.axis_size("space")):
        for r in range(count):
            axis, bit = routes()[r & 1][stage]
            ps, pr = (s ^ 1 << bit, r) if axis == "space" else (s, r ^ 1 << bit)
            route.append((s * count + r, ps * count + pr))
    return lax.ppermute(block, ("space", "rep"), route)


def side_of(stage):
    sides = [lax.axis_index(axis) >> bit & 1 for axis, bit in (r[stage] for r in routes())]
    return jnp.where(lax.axis_index("rep") & 1 == 0, sides[0], sides[1])


def summed(keep, give):
    block = keep + other_core(give)
    rows = block.shape[0] // 2
    upper = side_of(0) == 1
    low, high = block[:rows], block[rows:]
    block = jnp.where(upper, high, low) + swapped(jnp.where(upper, low, high), 0)
    for stage in range(1, len(routes()[0])):
        block = block + swapped(block, stage)
    other = swapped(block, 0)
    return jnp.where(
        upper, jnp.concatenate([other, block], 0), jnp.concatenate([block, other], 0)
    )


def body(features, neighbours, counts, cotangent, conv_weight, down_weight):
    slots, ch, vox = features.shape
    strips = lax.axis_size("space")
    faces = jnp.concatenate([features[:, :, :64], features[:, :, vox - 64 :]], 2)
    near = lax.ppermute(faces, "space", [(i, i ^ 1) for i in range(strips) if i ^ 1 < strips])
    steps = [(i, i + 1) for i in range(1, strips - 1, 2)]
    far = lax.ppermute(faces, "space", steps + [(b, a) for a, b in steps])
    place = jnp.stack([lax.axis_index("space") & 1, lax.axis_index("rep") & 1]).astype(jnp.int32)
    vmem = pl.BlockSpec(memory_space=pltpu.VMEM)
    smem = pl.BlockSpec(memory_space=pltpu.SMEM)
    taps, outs, _ = down_weight.shape
    total = conv_weight.size + down_weight.size
    rows = -(-total // (LANES * 128)) * 128
    part = jax.ShapeDtypeStruct((rows // 4, LANES), F32)
    hidden, keep_a, give_a, keep_b, give_b = pl.pallas_call(
        section_kernel,
        out_shape=(jax.ShapeDtypeStruct((slots, ch, vox), BF16), part, part, part, part),
        in_specs=[smem] * 3 + [vmem] * 6,
        out_specs=(vmem,) * 5,
        scratch_shapes=[
            pltpu.VMEM((slots + 1, 8, 8, 8, LANES), F32),
            pltpu.VMEM((2 * slots + 1, 8, 8, LANES), F32),
            pltpu.VMEM((2 * slots + 1, 8, 8, LANES), F32),
            pltpu.VMEM((slots, 10, 80, 2 * LANES), BF16),
            pltpu.VMEM((slots, 10, 64, 2 * LANES), BF16),
            pltpu.VMEM((3, 3 * ch, 2 * LANES), BF16),
            pltpu.VMEM((slots * ch, vox), F32),
            pltpu.VMEM((3 * ch, slots * 640), BF16),
            pltpu.VMEM((rows, LANES), F32),
        ],
        compiler_params=pltpu.CompilerParams(vmem_limit_bytes=32 << 20),
        name="section",
    )(
        neighbours, counts, place, features, near, far, cotangent, conv_weight,
        jnp.swapaxes(down_weight, 1, 2),
    )
    mine_a = summed(keep_a, give_a)
    mine_b = summed(keep_b, give_b)
    conv_grad, down_grad = pl.pallas_call(
        unpack_kernel,
        out_shape=(
            jax.ShapeDtypeStruct(conv_weight.shape, F32),
            jax.ShapeDtypeStruct((taps, ch, outs), F32),
        ),
        in_specs=[smem] + [vmem] * 4,
        out_specs=(vmem, vmem),
        scratch_shapes=[pltpu.VMEM((rows, LANES), F32)],
        compiler_params=pltpu.CompilerParams(vmem_limit_bytes=16 << 20),
        name="unpack",
    )(place, mine_a, other_core(mine_a), mine_b, other_core(mine_b))
    return hidden, conv_grad, jnp.swapaxes(down_grad, 1, 2)


def solution(mesh):
    return jax.shard_map(
        body,
        mesh=mesh,
        in_specs=(
            P(("space", "rep"), None, None),
            P(("space", "rep"), None),
            P(("space", "rep")),
            P(("space", "rep"), None, None),
            P(),
            P(),
        ),
        out_specs=(P(("space", "rep"), None, None), P(), P()),
        check_vma=False,
    )
```

```python
import functools

import jax
import jax.numpy as jnp
from jax import lax
from jax.experimental import pallas as pl
from jax.experimental.pallas import tpu as pltpu
from jax.sharding import PartitionSpec as P


F32 = jnp.float32
BF16 = jnp.bfloat16
LANES = 128


def dot(a, b, dims):
    return lax.dot_general(a, b, (dims, ((), ())), preferred_element_type=F32)


def lane_iota(shape):
    return lax.broadcasted_iota(jnp.int32, shape, len(shape) - 1)


def doubled(rows):
    return jnp.concatenate([rows, rows], 0).astype(F32).T


def regroup(blocks, outer, inner):
    ch = half = 64
    low = lane_iota((ch, LANES)) < half

    rows = []
    for j in range(inner):
        tiles = []
        for m in range(outer // 2):
            a = blocks[2 * m * ch : (2 * m + 1) * ch, j // 2 * LANES : (j // 2 + 1) * LANES]
            b = blocks[(2 * m + 1) * ch : (2 * m + 2) * ch, j // 2 * LANES : (j // 2 + 1) * LANES]
            if j % 2 == 0:
                tiles.append(jnp.where(low, a, pltpu.roll(b, half, 1)))
            else:
                tiles.append(jnp.where(low, pltpu.roll(a, half, 1), b))
        rows.append(jnp.concatenate(tiles, 1))
    return jnp.concatenate(rows, 0)


def weights_kernel(cw_ref, cot_ref, dw_ref, wn_ref, onehot_ref, hp_ref):
    ch, vox = cw_ref.shape[-1], onehot_ref.shape[0]
    slots = cot_ref.shape[0]
    half = ch

    low_lanes = lane_iota((ch, LANES)) < half
    for iy in range(3):
        for ix in range(3):
            parts = []
            for iz in range(3):
                w = cw_ref[ix * 9 + iy * 3 + iz].astype(F32)
                parts.append(jnp.concatenate([w, jnp.zeros_like(w)], 1))
            both = jnp.where(low_lanes, parts[0], pltpu.roll(parts[1], half, 1))
            wn_ref[iy, pl.ds(ix * ch, ch), pl.ds(0, LANES)] = both.astype(BF16)
            wn_ref[iy, pl.ds(ix * ch, ch), pl.ds(LANES, LANES)] = parts[2].astype(BF16)

    row = lax.broadcasted_iota(jnp.int32, (vox, LANES), 0)
    t, u = row // 64, row % 64
    voxel = (
        64 * (2 * (u // 16) + t // 4)
        + 8 * (2 * (u // 4 % 4) + t // 2 % 2)
        + 2 * (u % 4) + t % 2
    )
    lane = lane_iota((vox, LANES))
    for q in range(vox // LANES):
        hot = jnp.where(voxel == lane + q * LANES, 1.0, 0.0)
        onehot_ref[:, pl.ds(q * LANES, LANES)] = hot.astype(BF16)

    cot = cot_ref[...].reshape(slots * 64, LANES)
    taps = dw_ref.shape[0]
    hg = dot(dw_ref[...].reshape(taps * ch, LANES), cot, ((1,), (1,)))

    hg = regroup(hg, taps, slots).astype(BF16)
    hp_ref[...] = dot(hg, onehot_ref[...], ((1,), (0,))).astype(BF16)


def section_kernel(
    info_ref, feat_ref, near_ref, far_ref, cot_ref, wn_ref, onehot_ref, hp_ref,
    hid_ref, keep_a_ref, give_a_ref, keep_b_ref, give_b_ref,
    t0_ref, tl_ref, th_ref, sa_ref, sb_ref, as_ref, grad_ref,
):
    slots, ch, vox = feat_ref.shape
    half = ch
    odd, core = info_ref[0], info_ref[1]

    t0_ref[slots] = jnp.zeros(t0_ref.shape[1:], F32)
    tl_ref[2 * slots] = jnp.zeros(tl_ref.shape[1:], F32)
    th_ref[2 * slots] = jnp.zeros(th_ref.shape[1:], F32)
    for j in range(slots):
        block = doubled(feat_ref[j]).reshape(8, 8, 8, LANES)
        t0_ref[j] = block
        tl_ref[j] = block[7]
        th_ref[j] = block[0]
    near = near_ref[...].reshape(LANES, LANES).astype(F32).T
    far = far_ref[...].reshape(LANES, LANES).astype(F32).T
    narrow = lane_iota((64, LANES)) < half
    for side, table in ((1, tl_ref), (0, th_ref)):
        planes = jnp.where(odd == side, near, far)
        turned = pltpu.roll(planes, half, 1)
        for j in range(slots):
            rows = slice(j // 2 * 64, (j // 2 + 1) * 64)
            a, b = (planes, turned) if j % 2 == 0 else (turned, planes)
            table[slots + j] = jnp.where(narrow, a[rows], b[rows]).reshape(8, 8, LANES)

    cot = cot_ref[...].reshape(slots * 64, LANES)

    zi = lax.broadcasted_iota(jnp.int32, (10, 8, LANES), 1)
    li = lane_iota((10, 8, LANES))
    for j in range(slots):
        for xp in range(10):
            ox = -1 if xp == 0 else (1 if xp == 9 else 0)
            shifted = []
            for oz in (-1, 0, 1):
                pieces = []
                for oy in (-1, 0, 1):
                    col = (ox + 1) * 9 + (oy + 1) * 3 + oz + 1
                    if col == 13:
                        n = jnp.where(j < info_ref[2], j, slots)
                    else:
                        n = info_ref[3 + j * 27 + col]
                        n = jnp.where(n < 0, slots if ox == 0 else 2 * slots, n)
                    ys = slice(7, 8) if oy < 0 else (slice(0, 1) if oy > 0 else slice(0, 8))
                    if ox == 0:
                        pieces.append(t0_ref[n, xp - 1, ys])
                    elif ox < 0:
                        pieces.append(tl_ref[n, ys])
                    else:
                        pieces.append(th_ref[n, ys])
                shifted.append(jnp.concatenate(pieces, 0))
            below, here, above = shifted
            zm = pltpu.roll(jnp.where(zi == 7, below, here), 1, 1)
            zp = pltpu.roll(jnp.where(zi == 0, above, here), 7, 1)
            s01 = jnp.where(li < half, zm, here)
            sa_ref[j, xp, :, pl.ds(0, LANES)] = s01.reshape(80, LANES).astype(BF16)
            sa_ref[j, xp, :, pl.ds(LANES, LANES)] = zp.reshape(80, LANES).astype(BF16)
            sb_ref[j, xp, :, pl.ds(0, LANES)] = s01[1:9].reshape(64, LANES).astype(BF16)
            sb_ref[j, xp, :, pl.ds(LANES, LANES)] = zp[1:9].reshape(64, LANES).astype(BF16)

    def window(iy, first, count):
        if iy == 1:
            s = sb_ref[pl.ds(first, count)]
        else:
            s = sa_ref[pl.ds(first, count), :, pl.ds(8 * iy, 64)]
        return s.reshape(count * 640, 2 * LANES)

    zero = jnp.zeros((ch, LANES), F32)
    wide = lane_iota((vox, LANES)) < half
    for pair in range(slots // 2):
        sums = []
        for j in (2 * pair, 2 * pair + 1):
            out = dot(window(0, j, 1), wn_ref[0], ((1,), (1,)))
            out = out + dot(window(1, j, 1), wn_ref[1], ((1,), (1,)))
            out = out + dot(window(2, j, 1), wn_ref[2], ((1,), (1,)))
            mid = out[64 : 64 + vox, :LANES]
            last = out[128 : 128 + vox, LANES:]
            ends = out[:vox, :LANES] + jnp.concatenate([last, jnp.zeros((vox, LANES - ch), F32)], 1)
            sums.append((ends, mid))
        both = jnp.where(
            wide,
            sums[0][0] + pltpu.roll(sums[0][1], half, 1),
            pltpu.roll(sums[1][0], half, 1) + sums[1][1],
        ).T
        for j in (2 * pair, 2 * pair + 1):
            pre = both[j % 2 * ch : (j % 2 + 1) * ch]
            hid_ref[j] = jnp.maximum(pre, 0.0).astype(BF16)
            act = jnp.where(pre > 0, hp_ref[pl.ds(j * ch, ch), :].astype(F32), 0.0)
            lead = jnp.concatenate([act, zero], 1)
            cols = pl.ds(j * 640, 640)
            as_ref[pl.ds(0, ch), cols] = lead.astype(BF16)
            as_ref[pl.ds(ch, ch), cols] = pltpu.roll(lead, half, 1).astype(BF16)
            as_ref[pl.ds(2 * ch, ch), cols] = jnp.concatenate([zero, act], 1).astype(BF16)

    taps = vox // 64
    hidden = hid_ref[...].reshape(slots * ch, vox)
    hperm = dot(hidden, onehot_ref[...], ((1,), (1,)))
    hperm = regroup(hperm, slots, taps).astype(BF16)
    base = 3 * 3 * ch + 3 * ch + 3 * ch // 2
    grad_ref[pl.ds(base, taps * ch), :] = dot(hperm, cot, ((1,), (0,)))

    tails = []
    for iy in range(3):
        g = dot(as_ref[...], window(iy, 0, slots), ((1,), (0,)))
        grad_ref[pl.ds(iy * 3 * ch, 3 * ch), :] = g[:, :LANES]
        tails.append(g[:, LANES:])
    wide = lane_iota((3 * ch, LANES)) < half
    grad_ref[pl.ds(9 * ch, 3 * ch), :] = jnp.where(wide, tails[0], tails[1])
    hrows = 3 * ch // 2
    grad_ref[pl.ds(12 * ch, hrows), :] = jnp.where(wide[:hrows], tails[2][:hrows], tails[2][hrows:])
    used = base + taps * ch
    grad_ref[pl.ds(used, grad_ref.shape[0] - used), :] = jnp.zeros((grad_ref.shape[0] - used, LANES), F32)

    rows = keep_a_ref.shape[0]
    mine, theirs = pl.multiple_of(core * rows, 8), pl.multiple_of((1 - core) * rows, 8)
    keep_a_ref[...] = grad_ref[pl.ds(mine, rows), :]
    give_a_ref[...] = grad_ref[pl.ds(theirs, rows), :]
    keep_b_ref[...] = grad_ref[pl.ds(2 * rows + mine, rows), :]
    give_b_ref[...] = grad_ref[pl.ds(2 * rows + theirs, rows), :]


def unpack_kernel(info_ref, mine_a, other_a, mine_b, other_b, conv_ref, down_ref, x_ref):
    taps, ch, outs = down_ref.shape
    half = ch
    core = info_ref[1]
    rows = mine_a.shape[0]
    mine, theirs = pl.multiple_of(core * rows, 8), pl.multiple_of((1 - core) * rows, 8)
    x_ref[pl.ds(mine, rows), :] = mine_a[...]
    x_ref[pl.ds(theirs, rows), :] = other_a[...]
    x_ref[pl.ds(2 * rows + mine, rows), :] = mine_b[...]
    x_ref[pl.ds(2 * rows + theirs, rows), :] = other_b[...]
    base = 9 * ch + 3 * ch + 3 * ch // 2

    def put(ref, k, tile, upper):
        if upper:
            tile = pltpu.roll(tile, half, 1)
        ref[k] = tile[:, :ch]

    for iy in range(3):
        for ix in range(3):
            tile = x_ref[pl.ds(iy * 3 * ch + ix * ch, ch), :]
            put(conv_ref, ix * 9 + iy * 3, tile, False)
            put(conv_ref, ix * 9 + iy * 3 + 1, tile, True)
    for ix in range(3):
        tile = x_ref[pl.ds(9 * ch + ix * ch, ch), :]
        put(conv_ref, ix * 9 + 2, tile, False)
        put(conv_ref, ix * 9 + 5, tile, True)
    tail = x_ref[pl.ds(12 * ch, 3 * ch // 2), :]
    tail = jnp.concatenate([tail, pltpu.roll(tail, half, 1)], 0)
    for ix in range(3):
        conv_ref[ix * 9 + 8] = tail[ix * ch : (ix + 1) * ch, :ch]
    down_ref[...] = x_ref[pl.ds(base, taps * ch), :].reshape(taps, ch, outs)


def axis_bits(axis):
    return [(axis, b) for b in range(lax.axis_size(axis).bit_length() - 1)]


def routes():
    first = axis_bits("rep")[1:] + axis_bits("space")
    second = list(first)
    for i in range(0, len(second) - 1, 2):
        second[i], second[i + 1] = second[i + 1], second[i]
    return first, second


def other_core(block):
    return lax.ppermute(block, "rep", [(i, i ^ 1) for i in range(lax.axis_size("rep"))])


def swapped(block, stage):
    count = lax.axis_size("rep")
    route = []
    for s in range(lax.axis_size("space")):
        for r in range(count):
            axis, bit = routes()[r & 1][stage]
            ps, pr = (s ^ 1 << bit, r) if axis == "space" else (s, r ^ 1 << bit)
            route.append((s * count + r, ps * count + pr))
    return lax.ppermute(block, ("space", "rep"), route)


def side_of(stage):
    sides = [lax.axis_index(axis) >> bit & 1 for axis, bit in (r[stage] for r in routes())]
    return jnp.where(lax.axis_index("rep") & 1 == 0, sides[0], sides[1])


def summed(keep, give):
    block = keep + other_core(give)
    rows = block.shape[0] // 2
    upper = side_of(0) == 1
    low, high = block[:rows], block[rows:]
    block = jnp.where(upper, high, low) + swapped(jnp.where(upper, low, high), 0)
    for stage in range(1, len(routes()[0])):
        block = block + swapped(block, stage)
    other = swapped(block, 0)
    return jnp.where(
        upper, jnp.concatenate([other, block], 0), jnp.concatenate([block, other], 0)
    )


def body(features, neighbours, counts, cotangent, conv_weight, down_weight):
    slots, ch, vox = features.shape
    strips = lax.axis_size("space")
    taps, outs, _ = down_weight.shape
    odd = lax.axis_index("space") & 1
    core = lax.axis_index("rep") & 1

    own = jnp.stack([odd, core]).astype(jnp.int32)
    info = jnp.concatenate([own, counts, neighbours.reshape(-1)])

    pairs = slots // 2
    lower = jnp.concatenate([features[:pairs, :, :64], features[pairs:, :, :64]], 2)
    upper = jnp.concatenate([features[:pairs, :, vox - 64 :], features[pairs:, :, vox - 64 :]], 2)
    steps = [(i, i + 1) for i in range(0, strips - 1, 2)]
    near = lax.ppermute(jnp.where(odd == 1, lower, upper), "space", steps + [(b, a) for a, b in steps])
    steps = [(i, i + 1) for i in range(1, strips - 1, 2)]
    far = lax.ppermute(jnp.where(odd == 1, upper, lower), "space", steps + [(b, a) for a, b in steps])

    vmem = pl.BlockSpec(memory_space=pltpu.VMEM)
    smem = pl.BlockSpec(memory_space=pltpu.SMEM)
    weights, onehot, mixed = pl.pallas_call(
        weights_kernel,
        out_shape=(
            jax.ShapeDtypeStruct((3, 3 * ch, 2 * LANES), BF16),
            jax.ShapeDtypeStruct((vox, vox), BF16),
            jax.ShapeDtypeStruct((slots * ch, vox), BF16),
        ),
        in_specs=[vmem] * 3,
        out_specs=(vmem,) * 3,
        compiler_params=pltpu.CompilerParams(vmem_limit_bytes=16 << 20),
        cost_estimate=pl.CostEstimate(flops=10**9, bytes_accessed=10**6, transcendentals=0),
        name="weights",
    )(conv_weight, cotangent, jnp.swapaxes(down_weight, 1, 2))
    total = conv_weight.size + down_weight.size
    rows = -(-total // (LANES * 128)) * 128
    part = jax.ShapeDtypeStruct((rows // 4, LANES), F32)
    hidden, keep_a, give_a, keep_b, give_b = pl.pallas_call(
        section_kernel,
        out_shape=(jax.ShapeDtypeStruct((slots, ch, vox), BF16), part, part, part, part),
        in_specs=[smem] + [vmem] * 7,
        out_specs=(vmem,) * 5,
        scratch_shapes=[
            pltpu.VMEM((slots + 1, 8, 8, 8, LANES), F32),
            pltpu.VMEM((2 * slots + 1, 8, 8, LANES), F32),
            pltpu.VMEM((2 * slots + 1, 8, 8, LANES), F32),
            pltpu.VMEM((slots, 10, 80, 2 * LANES), BF16),
            pltpu.VMEM((slots, 10, 64, 2 * LANES), BF16),
            pltpu.VMEM((3 * ch, slots * 640), BF16),
            pltpu.VMEM((rows, LANES), F32),
        ],
        compiler_params=pltpu.CompilerParams(vmem_limit_bytes=32 << 20),
        name="section",
    )(
        info, features, near, far, cotangent, weights, onehot, mixed,
    )
    mine_a = summed(keep_a, give_a)
    mine_b = summed(keep_b, give_b)
    conv_grad, down_grad = pl.pallas_call(
        unpack_kernel,
        out_shape=(
            jax.ShapeDtypeStruct(conv_weight.shape, F32),
            jax.ShapeDtypeStruct((taps, ch, outs), F32),
        ),
        in_specs=[smem] + [vmem] * 4,
        out_specs=(vmem, vmem),
        scratch_shapes=[pltpu.VMEM((rows, LANES), F32)],
        compiler_params=pltpu.CompilerParams(vmem_limit_bytes=16 << 20),
        name="unpack",
    )(info, mine_a, other_core(mine_a), mine_b, other_core(mine_b))
    return hidden, conv_grad, jnp.swapaxes(down_grad, 1, 2)


def solution(mesh):
    return jax.shard_map(
        body,
        mesh=mesh,
        in_specs=(
            P(("space", "rep"), None, None),
            P(("space", "rep"), None),
            P(("space", "rep")),
            P(("space", "rep"), None, None),
            P(),
            P(),
        ),
        out_specs=(P(("space", "rep"), None, None), P(), P()),
        check_vma=False,
    )
```
